128 devices in a mesh: seq: 16 (over x_lo, z, core), fsdp: 8 (over x_hi, y).
Axes of the slice: x: 4 (x_hi: 2, x_lo: 2; x = x_hi * 2 + x_lo), y: 4, z: 4, core: 2. Of those that a mesh axis runs over, the one named last changes fastest.
Arguments:
- queries: bfloat16 [8, 4096, 4096], P('fsdp', 'seq'), may hold values from -60 to 60
- keys: bfloat16 [8, 4096, 4096], P('fsdp', 'seq'), may hold values from -4.8 to 4.8
- values: bfloat16 [8, 4096, 4096], P('fsdp', 'seq'), may hold values from -6 to 6
- out_weight: bfloat16 [4096, 3072], P(('seq', 'fsdp')), may hold values from -0.75 to 0.75
- block_lists: int32 [8, 32, 32, 8], P('fsdp'), may hold values from 0 to 31, as said below
- block_counts: int32 [8, 32, 32], P('fsdp'), may hold values from 1 to 8, as said below
Outputs:
- projected: bfloat16 [8, 4096, 3072], P('fsdp', 'seq')
The draws below stay inside these ranges and needn't reach their ends.
Inputs may be any that keep to these rules, and one draw needn't show every extreme that they name: `block_lists`: entry j = 0 of every list is the query block itself; the 8 entries of a list are distinct blocks; entries at slots j >= block_counts are ignored. `block_counts`: in every sequence some head and query block has 8 live slots.
All inputs are finite; a program needn't handle non-finite values.
Results may differ from the reference program's by a relative error of at most 0.0085.
Values may be sent and summed in bfloat16 or wider, within the bound.
A program may use at most 128 MiB of HBM per device.

```python
import jax
import jax.numpy as jnp
from jax import lax

HEADS = 32
HDIM = 128
DOUT = 3072
BLOCK = 128
KMAX = 8
SEQS = 8
LEN = 4096
QB = 32


def paired_fields(key):
    base_key = jax.random.fold_in(key, 11)
    first_key, second_key = jax.random.split(base_key)
    extent = (SEQS, LEN, HEADS * HDIM)
    key_field = jnp.clip(1.2 * jax.random.normal(first_key, extent, jnp.float32), -4.75, 4.75)
    query_field = jnp.clip(1.2 * jax.random.normal(second_key, extent, jnp.float32), -4.75, 4.75)
    return (query_field, key_field)


def draw_queries(key, part):
    return paired_fields(key)[0].astype(jnp.bfloat16)


def draw_keys(key, part):
    return paired_fields(key)[1].astype(jnp.bfloat16)


def shuffle_one(subkey):
    return jax.random.permutation(subkey, QB - 1).astype(jnp.int32)


def draw_block_lists(key, part):
    base_key = jax.random.fold_in(key, 23)
    row_total = SEQS * HEADS * QB
    subkeys = jax.random.split(base_key, row_total)
    orders = jax.vmap(shuffle_one)(subkeys)
    own_block = (jnp.arange(row_total, dtype=jnp.int32) % QB)[:, None]
    others = (own_block + 1 + orders[:, :KMAX - 1]) % QB
    listed = jnp.concatenate([own_block, others], axis=1)
    return listed.reshape(SEQS, HEADS, QB, KMAX).astype(jnp.int32)


def draw_block_counts(key, part):
    base_key = jax.random.fold_in(key, 37)
    cap_key, raw_key, head_key, block_key = jax.random.split(base_key, 4)
    ceilings = jax.random.randint(cap_key, (SEQS, HEADS, 1), 2, KMAX + 1, dtype=jnp.int32)
    raw_draw = jax.random.randint(raw_key, (SEQS, HEADS, QB), 0, 1 << 20, dtype=jnp.int32)
    counted = 1 + raw_draw % ceilings
    chosen_head = jax.random.randint(head_key, (SEQS, 1, 1), 0, HEADS, dtype=jnp.int32)
    chosen_block = jax.random.randint(block_key, (SEQS, 1, 1), 0, QB, dtype=jnp.int32)
    head_ids = lax.broadcasted_iota(jnp.int32, (SEQS, HEADS, QB), 1)
    block_ids = lax.broadcasted_iota(jnp.int32, (SEQS, HEADS, QB), 2)
    peak_spot = (head_ids == chosen_head) & (block_ids == chosen_block)
    return jnp.where(peak_spot, KMAX, counted).astype(jnp.int32)


def shard_levels(own_key, shape, cuts, smallest, high):
    factor_of = 1.0
    for axis_at, blocks in cuts:
        draws = jax.random.uniform(jax.random.fold_in(jax.random.fold_in(own_key, 6), axis_at), (blocks,), jnp.float32, smallest / len(cuts), high / len(cuts))
        factor_of = factor_of * jnp.repeat(jnp.exp(draws), shape[axis_at] // blocks).reshape((-1,) + (1,) * (len(shape) - 1 - axis_at))
    return factor_of


def gaussian(key, shape, width, reach, cuts=(), kind=jnp.bfloat16):
    entries = jax.random.normal(key, shape, jnp.float32) * width
    if len(cuts) > 0:
        entries = shard_levels(key, shape, cuts, -0.22, 0.18) * entries
    return jnp.clip(entries, min=-reach, max=reach).astype(kind)


def setup_inputs(seed: int = 0) -> dict:
    streams_of = jax.random.split(jax.random.key(seed), 7)
    queries = draw_queries(jax.random.fold_in(streams_of[6], 71), 0)
    keys = draw_keys(jax.random.fold_in(streams_of[6], 71), 0)
    values = gaussian(streams_of[2], (SEQS, LEN, HEADS * HDIM), 1.0, 6.0, ((0, 8), (1, 16)))
    out_weight = gaussian(streams_of[3], (HEADS * HDIM, DOUT), (HEADS * HDIM // 64) ** -0.5, 0.75, ((0, 128),))
    block_lists = draw_block_lists(jax.random.fold_in(streams_of[6], 71), 0)
    block_counts = draw_block_counts(jax.random.fold_in(streams_of[6], 71), 0)
    return dict(queries=queries, keys=keys, values=values, out_weight=out_weight, block_lists=block_lists, block_counts=block_counts)


def attend_one(operands):
    query_rows, key_rows, value_rows, block_ids, live_counts = operands
    query_blocks = query_rows.reshape(QB, BLOCK, HDIM).astype(jnp.float32)
    key_tiles = key_rows.reshape(QB, BLOCK, HDIM)[block_ids].reshape(QB, KMAX * BLOCK, HDIM).astype(jnp.float32)
    value_tiles = value_rows.reshape(QB, BLOCK, HDIM)[block_ids].reshape(QB, KMAX * BLOCK, HDIM).astype(jnp.float32)
    scores = jnp.einsum('qpd,qkd->qpk', query_blocks, key_tiles) * (HDIM ** -0.5)
    usable = jnp.arange(KMAX, dtype=jnp.int32)[None, :] < live_counts[:, None]
    usable = jnp.repeat(usable, BLOCK, axis=1)[:, None, :]
    scores = jnp.where(usable, scores, -jnp.inf)
    weights = jnp.exp(scores - jnp.max(scores, axis=2, keepdims=True))
    totals = jnp.sum(weights, axis=2, keepdims=True)
    rounded = lax.optimization_barrier(weights.astype(jnp.bfloat16)).astype(jnp.float32)
    mixed = jnp.einsum('qpk,qkd->qpd', rounded, value_tiles) / totals
    return mixed.astype(jnp.bfloat16).reshape(LEN, HDIM)


def split_heads(field):
    return field.reshape(SEQS, LEN, HEADS, HDIM).transpose(0, 2, 1, 3).reshape(SEQS * HEADS, LEN, HDIM)


def reference(queries, keys, values, out_weight, block_lists, block_counts):
    attended = lax.map(attend_one, (split_heads(queries), split_heads(keys), split_heads(values),
                                    block_lists.reshape(SEQS * HEADS, QB, KMAX),
                                    block_counts.reshape(SEQS * HEADS, QB)))
    attended = attended.reshape(SEQS, HEADS, LEN, HDIM).transpose(0, 2, 1, 3).reshape(SEQS * LEN, HEADS * HDIM)
    projected = jnp.dot(attended, out_weight, preferred_element_type=jnp.float32).astype(jnp.bfloat16)
    return projected.reshape(SEQS, LEN, DOUT)
```

```python
import functools
import math

import jax
import jax.numpy as jnp
from jax import lax
from jax.experimental import pallas as pl
from jax.experimental.pallas import tpu as pltpu
from jax.sharding import PartitionSpec as P

MESH = pl.DeviceIdType.MESH
PARTS = dict(a2a=True, gather=True, attend=True, project=True)


def kernel(
    lists, counts, q_hbm, k_hbm, v_hbm, w_hbm, out_hbm,
    q0, q1, k0, k1, v0, v1, sent, rows, wb, outv,
    in_sems, out_sems, own_sem, w_recv, w_send, sib_recv, sib_send,
    back_recv, back_send,
):
    seq = lax.axis_index("seq")
    fs = lax.axis_index("fsdp")
    xl, z, c = seq // 8, (seq // 2) % 4, seq % 2
    xh, y = fs // 4, fs % 4
    qb, kb, vb = (q0, q1), (k0, k1), (v0, v1)
    heads, blocks, dim = len(qb), q0.shape[0], q0.shape[2]
    span = q_hbm.shape[1]
    per = span // q0.shape[1]

    def seq_of(a, b, d):
        return (a * 4 + b) * 2 + d

    up, down = xh * 4 + (y + 1) % 4, xh * 4 + (y + 3) % 4
    opp = xh * 4 + (y + 2) % 4
    far = (1 - xh) * 4
    x_peer = (seq_of(1 - xl, z, c), fs)
    far_peer = (seq_of(1 - xl, z, c), far + y)
    sibling = (seq_of(xl, z, 1 - c), fs)
    up_peer, down_peer = (seq, up), (seq, down)

    barrier = pltpu.get_barrier_semaphore()
    for d in range(1, 16):
        pl.semaphore_signal(barrier, inc=1, device_id=((seq + d) % 16, fs), device_id_type=MESH)
    for peer in (far_peer, up_peer, down_peer):
        pl.semaphore_signal(barrier, inc=1, device_id=peer, device_id_type=MESH)
    pl.semaphore_wait(barrier, 18)

    pending = []

    def send(src, dst, ssem, rsem, peer):
        copy = pltpu.make_async_remote_copy(
            src_ref=src, dst_ref=dst, send_sem=ssem, recv_sem=rsem,
            device_id=peer, device_id_type=MESH,
        )
        copy.start()
        return copy

    def arrived(ref, sem):
        pltpu.make_async_copy(ref, ref, sem).wait()

    if PARTS["gather"]:
        own = wb.at[xl, z, c, fs]
        own_copy = pltpu.make_async_copy(w_hbm, own, own_sem.at[0])
        own_copy.start()
        for d in range(1, 4):
            pending.append(send(w_hbm, own, w_send.at[d], w_recv.at[0], (seq_of(xl, (z + d) % 4, c), fs)))

    order = [(dx, dz, dc) for dz in (2, 1, 3, 0) for dx in (1, 0) for dc in (1, 0)][:-1]

    def scatter(hbm, buf, t, h):
        for dx, dz, dc in order:
            p = seq_of((xl + dx) % 2, (z + dz) % 4, (c + dc) % 2)
            for part in range(per):
                rows_at = pl.ds(part * dim, dim)
                send(
                    hbm.at[0, rows_at, pl.ds(p * heads * dim + h * dim, dim)],
                    buf[h].at[seq * per + part],
                    out_sems.at[t, h], in_sems.at[t, h], (p, fs),
                )
        for part in range(per):
            pltpu.make_async_copy(
                hbm.at[0, pl.ds(part * dim, dim), pl.ds(seq * heads * dim + h * dim, dim)],
                buf[h].at[seq * per + part], in_sems.at[t, h],
            ).start()

    def scattered(buf, t, h):
        arrived(buf[h], in_sems.at[t, h])

    streams = ((k_hbm, kb), (q_hbm, qb), (v_hbm, vb))
    if PARTS["a2a"]:
        for t, (hbm, buf) in enumerate(streams):
            scatter(hbm, buf, t, 0)

    def piece(which, j):
        return wb.at[xl if which == 0 else 1 - xl, :, c, j]

    def to_sibling(view, n):
        pending.append(send(view, view, sib_send.at[n], sib_recv.at[n], sibling))

    def start_blocks(p):
        view = piece(p, fs)
        for kind, peer in ((0, up_peer), (1, down_peer), (2, far_peer)):
            n = 5 + p * 8 + kind
            pending.append(send(view, view, w_send.at[n], w_recv.at[2 + p * 8 + kind], peer))
        to_sibling(view, p * 8)

    def half(view, n):
        return view.at[pl.ds(2 * n, 2)]

    def relay_blocks(p):
        base = 2 + p * 8
        sbase = 5 + p * 8
        below, above = piece(p, down), piece(p, up)
        arrived(below, w_recv.at[base])
        pending.append(send(half(below, 0), half(below, 0), w_send.at[sbase + 3], w_recv.at[base + 3], up_peer))
        to_sibling(below, p * 8 + 1)
        arrived(above, w_recv.at[base + 1])
        pending.append(send(half(above, 1), half(above, 1), w_send.at[sbase + 4], w_recv.at[base + 4], down_peer))
        to_sibling(above, p * 8 + 2)
        across = piece(1 - p, far + y)
        arrived(across, w_recv.at[base + 2])
        pending.append(send(across, across, w_send.at[sbase + 5], w_recv.at[base + 5], up_peer))
        pending.append(send(across, across, w_send.at[sbase + 6], w_recv.at[base + 6], down_peer))
        to_sibling(across, p * 8 + 3)

    def last_blocks(p):
        base = 2 + p * 8
        sbase = 5 + p * 8
        facing = piece(p, opp)
        arrived(half(facing, 0), w_recv.at[base + 3])
        arrived(half(facing, 1), w_recv.at[base + 4])
        pending.append(send(facing, facing, w_send.at[sbase + 7], w_recv.at[base + 7], far_peer))
        to_sibling(facing, p * 8 + 4)

    def finish_blocks(p):
        base = 2 + p * 8
        q = 1 - p
        a, b, d = piece(q, far + (y + 3) % 4), piece(q, far + (y + 1) % 4), piece(q, far + (y + 2) % 4)
        arrived(a, w_recv.at[base + 5])
        to_sibling(a, p * 8 + 5)
        arrived(b, w_recv.at[base + 6])
        to_sibling(b, p * 8 + 6)
        arrived(d, w_recv.at[base + 7])
        to_sibling(d, p * 8 + 7)

    if PARTS["gather"]:
        own_copy.wait()
        arrived(wb.at[0, pl.ds(0, 3), c, 0], w_recv.at[0])
        pending.append(send(piece(0, fs), piece(0, fs), w_send.at[4], w_recv.at[1], x_peer))
        start_blocks(0)

    if PARTS["a2a"]:
        for t, (hbm, buf) in enumerate(streams):
            scatter(hbm, buf, t, 1)

    if PARTS["gather"]:
        arrived(piece(1, fs), w_recv.at[1])
        start_blocks(1)
        relay_blocks(0)
        last_blocks(0)

    scale = dim ** -0.5 * math.log2(math.e)

    def attend(h, i):
        base = (h * blocks + i) * 8
        live = counts[h * blocks + i]
        first = lists[base]
        q = qb[h][i]
        ids, bias = [], []
        for j in range(8):
            ids.append(jnp.where(j < live, lists[base + j], first))
            bias.append(jnp.where(j < live, 0.0, -jnp.inf).astype(jnp.float32))
        lane = lax.broadcasted_iota(jnp.int32, (1, 2 * dim), 1)
        scores = []
        for j in range(0, 8, 2):
            keys = jnp.concatenate([kb[h][ids[j]], kb[h][ids[j + 1]]], axis=0)
            scores.append(lax.dot_general(q, keys, (((1,), (1,)), ((), ())), preferred_element_type=jnp.float32))
        top = jnp.maximum(jnp.maximum(scores[0], scores[1]), jnp.maximum(scores[2], scores[3]))
        top = jnp.max(top, axis=1, keepdims=True) * scale
        total = None
        mixed = None
        for j in range(0, 8, 2):
            row = jnp.where(lane < dim, bias[j], bias[j + 1])
            weights = jnp.exp2((scores[j // 2] * scale - top) + row)
            values = jnp.concatenate([vb[h][ids[j]], vb[h][ids[j + 1]]], axis=0)
            part = jnp.dot(weights.astype(jnp.bfloat16), values, preferred_element_type=jnp.float32)
            total = weights if total is None else total + weights
            mixed = part if mixed is None else mixed + part
        total = jnp.sum(total, axis=1, keepdims=True)
        return (mixed / total).astype(jnp.bfloat16)

    def attend_head(h):
        def body(d, carry):
            p = (seq + d) % 16
            if PARTS["attend"]:
                for part in range(per):
                    sent[h, p, pl.ds(part * dim, dim), :] = attend(h, p * per + part)
            send(
                sent.at[h, p], rows.at[:, pl.ds(pl.multiple_of((seq * heads + h) * dim, dim), dim)],
                back_send.at[h], back_recv.at[h], (p, fs),
            )
            return carry

        lax.fori_loop(1, 16, body, 0)
        if PARTS["attend"]:
            for part in range(per):
                sent[h, seq, pl.ds(part * dim, dim), :] = attend(h, seq * per + part)
        pltpu.make_async_copy(
            sent.at[h, seq], rows.at[:, pl.ds(pl.multiple_of((seq * heads + h) * dim, dim), dim)],
            back_recv.at[h],
        ).start()

    if PARTS["a2a"]:
        for t, (hbm, buf) in enumerate(streams):
            scattered(buf, t, 0)
        attend_head(0)
    if PARTS["gather"]:
        relay_blocks(1)
        last_blocks(1)
        finish_blocks(0)
    if PARTS["a2a"]:
        for t, (hbm, buf) in enumerate(streams):
            scattered(buf, t, 1)
        attend_head(1)
    if PARTS["gather"]:
        finish_blocks(1)

    if PARTS["gather"]:
        for p in range(2):
            for n, (which, j) in enumerate((
                (p, fs), (p, down), (p, up), (1 - p, far + y), (p, opp),
                (1 - p, far + (y + 3) % 4), (1 - p, far + (y + 1) % 4), (1 - p, far + (y + 2) % 4),
            )):
                view = wb.at[xl if which == 0 else 1 - xl, :, 1 - c, j]
                arrived(view, sib_recv.at[p * 8 + n])
        for copy in pending:
            copy.wait_send()
    if PARTS["a2a"]:
        for h in range(heads):
            arrived(rows.at[:, pl.ds(0, 16 * dim)], back_recv.at[h])
            arrived(sent.at[h, pl.ds(0, 15)], back_send.at[h])
            for t, (hbm, buf) in enumerate(streams):
                arrived(buf[h].at[pl.ds(0, 15 * per)], out_sems.at[t, h])

    chunk = 256
    if PARTS["project"]:
        def project(n, carry):
            cols = pl.ds(pl.multiple_of(n * chunk, chunk), chunk)
            w = wb[:, :, :, :, :, cols].reshape(-1, chunk)
            outv[:, cols] = jnp.dot(rows[...], w, preferred_element_type=jnp.float32).astype(jnp.bfloat16)
            return carry

        lax.fori_loop(0, outv.shape[1] // chunk, project, 0)
    done = pltpu.make_async_copy(outv, out_hbm.at[0], own_sem.at[1])
    done.start()
    done.wait()


def shards(queries, keys, values, out_weight, block_lists, block_counts):
    seq = lax.axis_index("seq")
    groups = lax.axis_size("seq")
    others = lax.axis_size("fsdp")
    head_count = block_counts.shape[1]
    blocks = block_counts.shape[2]
    heads = head_count // groups
    span = queries.shape[1]
    dim = queries.shape[2] // head_count
    depth, width = out_weight.shape
    block = span * groups // blocks
    lists = lax.dynamic_slice_in_dim(block_lists[0], seq * heads, heads).reshape(-1)
    counts = lax.dynamic_slice_in_dim(block_counts[0], seq * heads, heads).reshape(-1)
    bf16 = jnp.bfloat16
    dma = pltpu.SemaphoreType.DMA
    hbm = pl.BlockSpec(memory_space=pl.ANY)
    smem = pl.BlockSpec(memory_space=pltpu.SMEM)
    head_buf = pltpu.VMEM((blocks, block, dim), bf16)
    return pl.pallas_call(
        kernel,
        out_shape=jax.ShapeDtypeStruct((1, span, width), bf16),
        in_specs=[smem, smem, hbm, hbm, hbm, hbm],
        out_specs=hbm,
        scratch_shapes=[
            *[head_buf] * (3 * heads),
            pltpu.VMEM((heads, groups, span, dim), bf16),
            pltpu.VMEM((span, head_count * dim), bf16),
            pltpu.VMEM((2, 4, 2, others, depth, width), bf16),
            pltpu.VMEM((span, width), bf16),
            dma((3, heads)), dma((3, heads)), dma((2,)),
            dma((18,)), dma((21,)), dma((16,)), dma((16,)),
            dma((heads,)), dma((heads,)),
        ],
        compiler_params=pltpu.CompilerParams(
            collective_id=0, has_side_effects=True, vmem_limit_bytes=60 << 20,
        ),
    )(lists, counts, queries, keys, values, out_weight)


def solution(mesh):
    return jax.shard_map(
        shards,
        mesh=mesh,
        in_specs=(
            P("fsdp", "seq", None),
            P("fsdp", "seq", None),
            P("fsdp", "seq", None),
            P(("seq", "fsdp"), None),
            P("fsdp", None, None, None),
            P("fsdp", None, None),
        ),
        out_specs=P("fsdp", "seq", None),
        check_vma=False,
    )
```

```python
import functools
import math

import jax
import jax.numpy as jnp
from jax import lax
from jax.experimental import pallas as pl
from jax.experimental.pallas import tpu as pltpu
from jax.sharding import PartitionSpec as P

MESH = pl.DeviceIdType.MESH
GROUP = 4
BOTH = (3,)
PARTS = dict(a2a=True, gather=True, attend=True, project=True)


def kernel(
    lists_hbm, counts_hbm, q_hbm, k_hbm, v_hbm, w_hbm, out_hbm,
    lists, counts, q0, q1, k0, k1, v0, v1, sent, rows, wb, acc, outv,
    in_sems, q_sems, out_sems, own_sem, w_recv, w_send, sib_recv, sib_send,
    back_recv, back_send,
):
    seq = lax.axis_index("seq")
    fs = lax.axis_index("fsdp")
    xl, z, c = seq // 8, (seq // 2) % 4, seq % 2
    xh, y = fs // 4, fs % 4
    qb, kb, vb = (q0, q1), (k0, k1), (v0, v1)
    heads, blocks, dim = len(qb), q0.shape[0], q0.shape[2]
    per = q_hbm.shape[0]
    span = per * dim

    def seq_of(a, b, d):
        return (a * 4 + b) * 2 + d

    up, down = xh * 4 + (y + 1) % 4, xh * 4 + (y + 3) % 4
    opp = xh * 4 + (y + 2) % 4
    far = (1 - xh) * 4
    x_peer = (seq_of(1 - xl, z, c), fs)
    far_peer = (seq_of(1 - xl, z, c), far + y)
    sibling = (seq_of(xl, z, 1 - c), fs)
    z_up, z_down = (z + 1) % 4, (z + 3) % 4
    z_opp = (z + 2) % 4
    up_peer, down_peer = (seq, up), (seq, down)

    barrier = pltpu.get_barrier_semaphore()
    for d in range(1, 16):
        pl.semaphore_signal(barrier, inc=1, device_id=((seq + d) % 16, fs), device_id_type=MESH)
    for peer in (far_peer, up_peer, down_peer):
        pl.semaphore_signal(barrier, inc=1, device_id=peer, device_id_type=MESH)
    fetched = [
        pltpu.make_async_copy(lists_hbm.at[0, pl.ds(seq * heads, heads)], lists, own_sem.at[2]),
        pltpu.make_async_copy(counts_hbm.at[0], counts, own_sem.at[3]),
    ]
    own = wb.at[xl, z, c, fs]
    if PARTS["gather"]:
        fetched.append(pltpu.make_async_copy(w_hbm, own, own_sem.at[0]))
    for copy in fetched:
        copy.start()
    for h in range(heads):
        vb[h][:blocks, :, dim:] = jnp.ones((blocks, dim, dim), jnp.bfloat16)
        vb[h][blocks] = jnp.zeros((dim, 2 * dim), jnp.bfloat16)
    for copy in fetched:
        copy.wait()
    pl.semaphore_wait(barrier, 18)

    pending = []

    def send(src, dst, ssem, rsem, peer):
        copy = pltpu.make_async_remote_copy(
            src_ref=src, dst_ref=dst, send_sem=ssem, recv_sem=rsem,
            device_id=peer, device_id_type=MESH,
        )
        copy.start()
        return copy

    def share(view, n, peer):
        pending.append(send(view, view, w_send.at[n], w_recv.at[n], peer))

    def arrived(ref, sem):
        pltpu.make_async_copy(ref, ref, sem).wait()

    def landing(buf, first, count):
        view = buf.at[pl.ds(first, count)]
        return view if buf.shape[2] == dim else view.at[:, :, pl.ds(0, dim)]

    order = [(dx, dz, dc) for dz in (2, 1, 3, 0) for dx in (1, 0) for dc in (1, 0)]

    def peer_at(n, way):
        dx, dz, dc = order[n]
        return seq_of((xl + dx) % 2, (z + 4 + way * dz) % 4, (c + dc) % 2)

    def scatter(hbm, buf, h, out_sem, in_sem):
        if not PARTS["a2a"]:
            return
        mine = landing(buf[h], seq * per, per)
        for n in range(16):
            p = peer_at(n, 1)
            block = hbm.at[:, :, pl.ds(pl.multiple_of((p * heads + h) * dim, dim), dim)]
            if n < 15:
                send(block, mine, out_sem, in_sem(n), (p, fs))
            else:
                pltpu.make_async_copy(block, mine, in_sem(n)).start()

    def scatter_k(h):
        scatter(k_hbm, kb, h, out_sems.at[0, h], lambda n: in_sems.at[0, h])

    def scatter_v(h):
        scatter(v_hbm, vb, h, out_sems.at[1, h], lambda n: in_sems.at[1, h])

    def scatter_q(h):
        scatter(q_hbm, qb, h, out_sems.at[2, h], lambda n: q_sems.at[h, n // GROUP])

    def scattered(h):
        if PARTS["a2a"]:
            arrived(landing(kb[h], 0, blocks), in_sems.at[0, h])
            arrived(landing(vb[h], 0, blocks), in_sems.at[1, h])

    def queries_in(h, g):
        if PARTS["a2a"]:
            arrived(qb[h].at[pl.ds(0, GROUP * per)], q_sems.at[h, g])

    def pair(d, j):
        return wb.at[:, (z + d) % 4, c, j]

    def to_sibling(d, kind, view):
        n = d * 8 + kind
        pending.append(send(view, view, sib_send.at[n], sib_recv.at[n], sibling))

    def slot(d, kind):
        return 8 + d * 10 + kind

    def blocks_out(d):
        view = pair(d, fs)
        if d > 0:
            for kind, peer in ((0, up_peer), (1, down_peer), (2, far_peer)):
                share(view, slot(d, kind), peer)
        to_sibling(d, 0, view)

    def arrived_pair(d, j, kind, flip):
        if d > 0:
            arrived(pair(d, j), w_recv.at[slot(d, kind)])
        else:
            first = 1 - xl if flip else xl
            arrived(wb.at[first, z, c, j], w_recv.at[5 + kind])
            arrived(wb.at[1 - first, z, c, j], w_recv.at[slot(0, kind)])

    def relay_y(d):
        below, above = pair(d, down), pair(d, up)
        arrived_pair(d, down, 0, False)
        share(below.at[0], slot(d, 3), up_peer)
        if d in BOTH:
            share(below.at[1], slot(d, 8), far_peer)
        to_sibling(d, 1, below)
        arrived_pair(d, up, 1, False)
        share(above.at[1], slot(d, 4), down_peer)
        if d in BOTH:
            share(above.at[0], slot(d, 9), far_peer)
        to_sibling(d, 2, above)

    def relay_far(d):
        across = pair(d, far + y)
        arrived_pair(d, far + y, 2, True)
        share(across.at[0] if d in BOTH else across, slot(d, 5), up_peer)
        share(across.at[1] if d in BOTH else across, slot(d, 6), down_peer)
        to_sibling(d, 3, across)

    def relay_opp(d):
        facing = pair(d, opp)
        arrived(facing.at[0], w_recv.at[slot(d, 3)])
        arrived(facing.at[1], w_recv.at[slot(d, 4)])
        share(facing, slot(d, 7), far_peer)
        to_sibling(d, 4, facing)

    def finish(d):
        low, high, last = (pair(d, far + (y + n) % 4) for n in (3, 1, 2))
        if d in BOTH:
            arrived(low.at[0], w_recv.at[slot(d, 5)])
            arrived(low.at[1], w_recv.at[slot(d, 8)])
            arrived(high.at[1], w_recv.at[slot(d, 6)])
            arrived(high.at[0], w_recv.at[slot(d, 9)])
        else:
            arrived(low, w_recv.at[slot(d, 5)])
            arrived(high, w_recv.at[slot(d, 6)])
        to_sibling(d, 5, low)
        to_sibling(d, 6, high)
        arrived(last, w_recv.at[slot(d, 7)])
        to_sibling(d, 7, last)

    def z_peer(zz):
        return (seq_of(xl, zz, c), fs)

    def gather_own():
        share(own, 0, x_peer)
        for kind, peer in ((0, up_peer), (1, down_peer), (2, far_peer)):
            share(own, 5 + kind, peer)

    def gather_x():
        other = wb.at[1 - xl, z, c, fs]
        arrived(other, w_recv.at[0])
        share(pair(0, fs), 1, z_peer(z_up))
        share(pair(0, fs), 2, z_peer(z_down))
        for kind, peer in ((0, up_peer), (1, down_peer), (2, far_peer)):
            share(other, slot(0, kind), peer)
        blocks_out(0)

    def gather_z():
        arrived(pair(3, fs), w_recv.at[1])
        share(wb.at[0, z_down, c, fs], 3, z_peer(z_up))
        arrived(pair(1, fs), w_recv.at[2])
        share(wb.at[1, z_up, c, fs], 4, z_peer(z_down))
        blocks_out(3)
        blocks_out(1)

    def gather_opp():
        arrived(wb.at[0, z_opp, c, fs], w_recv.at[3])
        arrived(wb.at[1, z_opp, c, fs], w_recv.at[4])
        blocks_out(2)

    def run(step, *args):
        if PARTS["gather"]:
            step(*args)

    scale = dim ** -0.5 * math.log2(math.e)

    def attend(h, i):
        live = counts[seq * heads + h, i]
        first = lists[h, i, 0]
        ids = [lists[h, i, j] for j in range(8)]
        key_ids = [jnp.where(j < live, ids[j], first) for j in range(8)]
        value_ids = [jnp.where(j < live, ids[j], blocks) for j in range(8)]
        q = qb[h][i]
        scores = []
        for j in range(0, 8, 2):
            keys = jnp.concatenate([kb[h][key_ids[j]], kb[h][key_ids[j + 1]]], axis=0)
            scores.append(lax.dot_general(q, keys, (((1,), (1,)), ((), ())), preferred_element_type=jnp.float32))
        top = jnp.maximum(jnp.maximum(scores[0], scores[1]), jnp.maximum(scores[2], scores[3]))
        top = jnp.max(jnp.maximum(top[:, :dim], top[:, dim:]), axis=1, keepdims=True)
        mixed = None
        for j in range(0, 8, 2):
            weights = jnp.exp2((scores[j // 2] - top) * scale).astype(jnp.bfloat16)
            values = jnp.concatenate([vb[h][value_ids[j]], vb[h][value_ids[j + 1]]], axis=0)
            part = jnp.dot(weights, values, preferred_element_type=jnp.float32)
            mixed = part if mixed is None else mixed + part
        return (mixed[:, :dim] / mixed[:, dim:]).astype(jnp.bfloat16)

    def attend_group(h, g):
        if not PARTS["a2a"]:
            return
        queries_in(h, g)
        peers = [peer_at(g * GROUP + n, -1) for n in range(GROUP)]
        if PARTS["attend"]:
            done = [[attend(h, p * per + part) for part in range(per)] for p in peers]
            for p, blocks_of in zip(peers, done):
                for part in range(per):
                    sent[h, p, pl.ds(part * dim, dim), :] = blocks_of[part]
        columns = pl.ds(pl.multiple_of((h * 16 + seq) * dim, dim), dim)
        for n, p in enumerate(peers):
            if g * GROUP + n < 15:
                send(sent.at[h, p], rows.at[:, columns], back_send.at[h], back_recv.at[h], (p, fs))
            else:
                pltpu.make_async_copy(sent.at[h, p], rows.at[:, columns], back_recv.at[h]).start()

    def returned(h):
        if PARTS["a2a"]:
            arrived(rows.at[:, pl.ds(h * 16 * dim, 16 * dim)], back_recv.at[h])

    def from_sibling():
        for d in range(4):
            for kind, j in enumerate((
                fs, down, up, far + y, opp, far + (y + 3) % 4, far + (y + 1) % 4, far + (y + 2) % 4,
            )):
                arrived(wb.at[:, (z + d) % 4, 1 - c, j], sib_recv.at[d * 8 + kind])

    chunk = 256
    others, depth = wb.shape[3], wb.shape[4]

    def project(h, last):
        if not PARTS["project"]:
            return
        lower = h * dim // depth
        near = pl.ds(lower, dim // depth)

        def body(n, carry):
            cols = pl.ds(pl.multiple_of(n * chunk, chunk), chunk)
            w = wb[:, :, :, near, :, cols].reshape(16 * dim, chunk)
            part = jnp.dot(rows[:, h * 16 * dim:(h + 1) * 16 * dim], w, preferred_element_type=jnp.float32)
            if h > 0:
                part = acc[:, cols] + part
            if last:
                outv[:, cols] = part.astype(jnp.bfloat16)
                pltpu.make_async_copy(outv.at[:, cols], out_hbm.at[0, :, cols], own_sem.at[1]).start()
            else:
                acc[:, cols] = part
            return carry

        lax.fori_loop(0, outv.shape[1] // chunk, body, 0)

    run(gather_own)
    run(gather_x)
    run(gather_z)
    scatter_k(0)
    run(gather_opp)
    scatter_v(0)
    scatter_q(0)
    run(relay_y, 0)
    run(relay_far, 0)
    scatter_k(1)
    scatter_v(1)
    scatter_q(1)
    run(relay_y, 3)
    run(relay_far, 3)
    run(relay_y, 1)
    run(relay_far, 1)
    run(relay_y, 2)
    run(relay_far, 2)
    run(relay_opp, 0)
    scattered(0)
    attend_group(0, 0)
    run(relay_opp, 3)
    attend_group(0, 1)
    run(relay_opp, 1)
    attend_group(0, 2)
    run(relay_opp, 2)
    attend_group(0, 3)
    run(finish, 0)
    run(finish, 3)
    scattered(1)
    attend_group(1, 0)
    attend_group(1, 1)
    attend_group(1, 2)
    attend_group(1, 3)
    run(finish, 1)
    run(finish, 2)
    run(from_sibling)
    returned(0)
    project(0, False)
    returned(1)
    project(1, True)
    if PARTS["gather"]:
        for copy in pending:
            copy.wait_send()
    if PARTS["a2a"]:
        for h in range(heads):
            arrived(sent.at[h, pl.ds(0, 15)], back_send.at[h])
            for t in range(3):
                arrived(qb[h].at[pl.ds(0, 15 * per)], out_sems.at[t, h])
    if PARTS["project"]:
        arrived(outv, own_sem.at[1])


def shards(queries, keys, values, out_weight, block_lists, block_counts):
    groups = lax.axis_size("seq")
    others = lax.axis_size("fsdp")
    head_count = block_counts.shape[1]
    blocks = block_counts.shape[2]
    heads = head_count // groups
    span = queries.shape[1]
    dim = queries.shape[2] // head_count
    depth, width = out_weight.shape
    block = span * groups // blocks
    bf16 = jnp.bfloat16
    dma = pltpu.SemaphoreType.DMA
    hbm = pl.BlockSpec(memory_space=pl.ANY)
    head_buf = pltpu.VMEM((blocks, block, dim), bf16)
    return pl.pallas_call(
        kernel,
        out_shape=jax.ShapeDtypeStruct((1, span, width), bf16),
        in_specs=[hbm] * 6,
        out_specs=hbm,
        scratch_shapes=[
            pltpu.SMEM((heads, blocks, block_lists.shape[3]), jnp.int32),
            pltpu.SMEM((head_count, blocks), jnp.int32),
            *[head_buf] * (2 * heads),
            *[pltpu.VMEM((blocks + 1, block, 2 * dim), bf16)] * heads,
            pltpu.VMEM((heads, groups, span, dim), bf16),
            pltpu.VMEM((span, head_count * dim), bf16),
            pltpu.VMEM((2, 4, 2, others, depth, width), bf16),
            pltpu.VMEM((span, width), jnp.float32),
            pltpu.VMEM((span, width), bf16),
            dma((2, heads)), dma((heads, groups // GROUP)), dma((3, heads)), dma((4,)),
            dma((48,)), dma((48,)), dma((32,)), dma((32,)),
            dma((heads,)), dma((heads,)),
        ],
        compiler_params=pltpu.CompilerParams(
            collective_id=0, has_side_effects=True, vmem_limit_bytes=60 << 20,
        ),
    )(block_lists, block_counts, *(a.reshape(-1, block, a.shape[2]) for a in (queries, keys, values)), out_weight)


def solution(mesh):
    return jax.shard_map(
        shards,
        mesh=mesh,
        in_specs=(
            P("fsdp", "seq", None),
            P("fsdp", "seq", None),
            P("fsdp", "seq", None),
            P(("seq", "fsdp"), None),
            P("fsdp", None, None, None),
            P("fsdp", None, None),
        ),
        out_specs=P("fsdp", "seq", None),
        check_vma=False,
    )
```

```python
import functools
import math

import jax
import jax.numpy as jnp
from jax import lax
from jax.experimental import pallas as pl
from jax.experimental.pallas import tpu as pltpu
from jax.sharding import PartitionSpec as P

MESH = pl.DeviceIdType.MESH
GROUP = 4
BOTH = (3,)
PARTS = dict(a2a=True, gather=True, attend=True, project=True)


def kernel(
    lists_hbm, counts_hbm, q_hbm, k_hbm, v_hbm, w_hbm, out_hbm,
    lists, counts, q0, q1, k0, k1, v0, v1, sent, rows, wb, acc, outv,
    in_sems, q_sems, out_sems, own_sem, w_recv, w_send, sib_recv, sib_send,
    back_recv, back_send,
):
    seq = lax.axis_index("seq")
    fs = lax.axis_index("fsdp")
    xl, z, c = seq // 8, (seq // 2) % 4, seq % 2
    xh, y = fs // 4, fs % 4
    qb, kb, vb = (q0, q1), (k0, k1), (v0, v1)
    heads, blocks, dim = len(qb), q0.shape[0], q0.shape[2]
    per = q_hbm.shape[0]
    span = per * dim

    def seq_of(a, b, d):
        return (a * 4 + b) * 2 + d

    up, down = xh * 4 + (y + 1) % 4, xh * 4 + (y + 3) % 4
    opp = xh * 4 + (y + 2) % 4
    far = (1 - xh) * 4
    x_peer = (seq_of(1 - xl, z, c), fs)
    far_peer = (seq_of(1 - xl, z, c), far + y)
    sibling = (seq_of(xl, z, 1 - c), fs)
    z_up, z_down = (z + 1) % 4, (z + 3) % 4
    z_opp = (z + 2) % 4
    up_peer, down_peer = (seq, up), (seq, down)

    barrier = pltpu.get_barrier_semaphore()
    for d in range(1, 16):
        pl.semaphore_signal(barrier, inc=1, device_id=((seq + d) % 16, fs), device_id_type=MESH)
    for peer in (far_peer, up_peer, down_peer):
        pl.semaphore_signal(barrier, inc=1, device_id=peer, device_id_type=MESH)
    fetched = [
        pltpu.make_async_copy(lists_hbm.at[0, pl.ds(seq * heads, heads)], lists, own_sem.at[2]),
        pltpu.make_async_copy(counts_hbm.at[0], counts, own_sem.at[3]),
    ]
    own = wb.at[xl, z, c, fs]
    if PARTS["gather"]:
        fetched.append(pltpu.make_async_copy(w_hbm, own, own_sem.at[0]))
    for copy in fetched:
        copy.start()
    for h in range(heads):
        vb[h][:blocks, :, dim:] = jnp.ones((blocks, dim, dim), jnp.bfloat16)
        vb[h][blocks] = jnp.zeros((dim, 2 * dim), jnp.bfloat16)
    for copy in fetched:
        copy.wait()
    pl.semaphore_wait(barrier, 18)

    pending = []

    def send(src, dst, ssem, rsem, peer):
        copy = pltpu.make_async_remote_copy(
            src_ref=src, dst_ref=dst, send_sem=ssem, recv_sem=rsem,
            device_id=peer, device_id_type=MESH,
        )
        copy.start()
        return copy

    def share(view, n, peer):
        pending.append(send(view, view, w_send.at[n], w_recv.at[n], peer))

    def arrived(ref, sem):
        pltpu.make_async_copy(ref, ref, sem).wait()

    def landing(buf, first, count):
        view = buf.at[pl.ds(first, count)]
        return view if buf.shape[2] == dim else view.at[:, :, pl.ds(0, dim)]

    order = [(dx, dz, dc) for dc in (1, 0) for dx in (1, 0) for dz in (2, 1, 3, 0)]

    def peer_at(n, way):
        dx, dz, dc = order[n]
        return seq_of((xl + dx) % 2, (z + 4 + way * dz) % 4, (c + dc) % 2)

    def scatter(hbm, buf, h, out_sem, in_sem, lo, hi):
        if not PARTS["a2a"]:
            return
        mine = landing(buf[h], seq * per, per)
        for n in range(lo, hi):
            p = peer_at(n, 1)
            block = hbm.at[:, :, pl.ds(pl.multiple_of((p * heads + h) * dim, dim), dim)]
            if n < 15:
                send(block, mine, out_sem, in_sem(n), (p, fs))
            else:
                pltpu.make_async_copy(block, mine, in_sem(n)).start()

    def scatter_k(h, lo=0, hi=16):
        scatter(k_hbm, kb, h, out_sems.at[0, h], lambda n: in_sems.at[0, h], lo, hi)

    def scatter_v(h, lo=0, hi=16):
        scatter(v_hbm, vb, h, out_sems.at[1, h], lambda n: in_sems.at[1, h], lo, hi)

    def scatter_q(h, lo=0, hi=16):
        scatter(q_hbm, qb, h, out_sems.at[2, h], lambda n: q_sems.at[h, n // GROUP], lo, hi)

    def scattered(h):
        if PARTS["a2a"]:
            arrived(landing(kb[h], 0, blocks), in_sems.at[0, h])
            arrived(landing(vb[h], 0, blocks), in_sems.at[1, h])

    def queries_in(h, g):
        if PARTS["a2a"]:
            arrived(qb[h].at[pl.ds(0, GROUP * per)], q_sems.at[h, g])

    def pair(d, j):
        return wb.at[:, (z + d) % 4, c, j]

    def to_sibling(d, kind, view):
        n = d * 8 + kind
        pending.append(send(view, view, sib_send.at[n], sib_recv.at[n], sibling))

    def slot(d, kind):
        return 8 + d * 10 + kind

    def blocks_out(d):
        view = pair(d, fs)
        if d > 0:
            for kind, peer in ((0, up_peer), (1, down_peer), (2, far_peer)):
                share(view, slot(d, kind), peer)
        to_sibling(d, 0, view)

    def arrived_pair(d, j, kind, flip):
        if d > 0:
            arrived(pair(d, j), w_recv.at[slot(d, kind)])
        else:
            first = 1 - xl if flip else xl
            arrived(wb.at[first, z, c, j], w_recv.at[5 + kind])
            arrived(wb.at[1 - first, z, c, j], w_recv.at[slot(0, kind)])

    def relay_y(d):
        below, above = pair(d, down), pair(d, up)
        arrived_pair(d, down, 0, False)
        share(below.at[0], slot(d, 3), up_peer)
        if d in BOTH:
            share(below.at[1], slot(d, 8), far_peer)
        to_sibling(d, 1, below)
        arrived_pair(d, up, 1, False)
        share(above.at[1], slot(d, 4), down_peer)
        if d in BOTH:
            share(above.at[0], slot(d, 9), far_peer)
        to_sibling(d, 2, above)

    def relay_far(d):
        across = pair(d, far + y)
        arrived_pair(d, far + y, 2, True)
        share(across.at[0] if d in BOTH else across, slot(d, 5), up_peer)
        share(across.at[1] if d in BOTH else across, slot(d, 6), down_peer)
        to_sibling(d, 3, across)

    def relay_opp(d):
        facing = pair(d, opp)
        arrived(facing.at[0], w_recv.at[slot(d, 3)])
        arrived(facing.at[1], w_recv.at[slot(d, 4)])
        share(facing, slot(d, 7), far_peer)
        to_sibling(d, 4, facing)

    def finish(d):
        low, high, last = (pair(d, far + (y + n) % 4) for n in (3, 1, 2))
        if d in BOTH:
            arrived(low.at[0], w_recv.at[slot(d, 5)])
            arrived(low.at[1], w_recv.at[slot(d, 8)])
            arrived(high.at[1], w_recv.at[slot(d, 6)])
            arrived(high.at[0], w_recv.at[slot(d, 9)])
        else:
            arrived(low, w_recv.at[slot(d, 5)])
            arrived(high, w_recv.at[slot(d, 6)])
        to_sibling(d, 5, low)
        to_sibling(d, 6, high)
        arrived(last, w_recv.at[slot(d, 7)])
        to_sibling(d, 7, last)

    def z_peer(zz):
        return (seq_of(xl, zz, c), fs)

    def gather_own():
        share(own, 0, x_peer)
        for kind, peer in ((0, up_peer), (1, down_peer), (2, far_peer)):
            share(own, 5 + kind, peer)

    def gather_x():
        other = wb.at[1 - xl, z, c, fs]
        arrived(other, w_recv.at[0])
        share(pair(0, fs), 1, z_peer(z_up))
        share(pair(0, fs), 2, z_peer(z_down))
        for kind, peer in ((0, up_peer), (1, down_peer), (2, far_peer)):
            share(other, slot(0, kind), peer)
        blocks_out(0)

    def gather_z():
        arrived(pair(3, fs), w_recv.at[1])
        share(wb.at[0, z_down, c, fs], 3, z_peer(z_up))
        arrived(pair(1, fs), w_recv.at[2])
        share(wb.at[1, z_up, c, fs], 4, z_peer(z_down))
        blocks_out(3)
        blocks_out(1)

    def gather_opp():
        arrived(wb.at[0, z_opp, c, fs], w_recv.at[3])
        arrived(wb.at[1, z_opp, c, fs], w_recv.at[4])
        blocks_out(2)

    def run(step, *args):
        if PARTS["gather"]:
            step(*args)

    scale = dim ** -0.5 * math.log2(math.e)

    def attend(h, i):
        live = counts[seq * heads + h, i]
        first = lists[h, i, 0]
        ids = [lists[h, i, j] for j in range(8)]
        key_ids = [jnp.where(j < live, ids[j], first) for j in range(8)]
        value_ids = [jnp.where(j < live, ids[j], blocks) for j in range(8)]
        q = qb[h][i]
        scores = []
        for j in range(0, 8, 2):
            keys = jnp.concatenate([kb[h][key_ids[j]], kb[h][key_ids[j + 1]]], axis=0)
            scores.append(lax.dot_general(q, keys, (((1,), (1,)), ((), ())), preferred_element_type=jnp.float32))
        top = jnp.maximum(jnp.maximum(scores[0], scores[1]), jnp.maximum(scores[2], scores[3]))
        top = jnp.max(jnp.maximum(top[:, :dim], top[:, dim:]), axis=1, keepdims=True)
        mixed = None
        for j in range(0, 8, 2):
            weights = jnp.exp2((scores[j // 2] - top) * scale).astype(jnp.bfloat16)
            values = jnp.concatenate([vb[h][value_ids[j]], vb[h][value_ids[j + 1]]], axis=0)
            part = jnp.dot(weights, values, preferred_element_type=jnp.float32)
            mixed = part if mixed is None else mixed + part
        return (mixed[:, :dim] / mixed[:, dim:]).astype(jnp.bfloat16)

    def attend_group(h, g):
        if not PARTS["a2a"]:
            return
        queries_in(h, g)
        peers = [peer_at(g * GROUP + n, -1) for n in range(GROUP)]
        if PARTS["attend"]:
            done = [[attend(h, p * per + part) for part in range(per)] for p in peers]
            for p, blocks_of in zip(peers, done):
                for part in range(per):
                    sent[h, p, pl.ds(part * dim, dim), :] = blocks_of[part]
        columns = pl.ds(pl.multiple_of((h * 16 + seq) * dim, dim), dim)
        for n, p in enumerate(peers):
            if g * GROUP + n < 15:
                send(sent.at[h, p], rows.at[:, columns], back_send.at[h], back_recv.at[h, g], (p, fs))
            else:
                pltpu.make_async_copy(sent.at[h, p], rows.at[:, columns], back_recv.at[h, g]).start()

    def returned(h, *groups):
        if PARTS["a2a"]:
            for g in groups:
                arrived(rows.at[:, pl.ds(0, GROUP * dim)], back_recv.at[h, g])

    def from_sibling():
        for d in range(4):
            for kind, j in enumerate((
                fs, down, up, far + y, opp, far + (y + 3) % 4, far + (y + 1) % 4, far + (y + 2) % 4,
            )):
                arrived(wb.at[:, (z + d) % 4, 1 - c, j], sib_recv.at[d * 8 + kind])

    chunk = 1024
    others, depth = wb.shape[3], wb.shape[4]

    def project(h, first, last):
        if not PARTS["project"]:
            return
        near = pl.ds(h * dim // depth, dim // depth)

        def body(n, carry):
            cols = pl.ds(pl.multiple_of(n * chunk, chunk), chunk)
            part = jnp.dot(
                rows[:, h * 16 * dim:(h + 1) * 16 * dim],
                wb[:, :, :, near, :, cols].reshape(16 * dim, chunk), preferred_element_type=jnp.float32,
            )
            if not first:
                part = acc[:, cols] + part
            if last:
                outv[:, cols] = part.astype(jnp.bfloat16)
                pltpu.make_async_copy(outv.at[:, cols], out_hbm.at[0, :, cols], own_sem.at[1]).start()
            else:
                acc[:, cols] = part
            return carry

        lax.fori_loop(0, outv.shape[1] // chunk, body, 0)

    run(gather_own)
    scatter_k(0)
    run(gather_x)
    scatter_v(0)
    run(gather_z)
    scatter_q(0)
    run(gather_opp)
    run(relay_y, 0)
    run(relay_far, 0)
    scatter_k(1)
    scatter_v(1)
    run(relay_y, 3)
    run(relay_far, 3)
    run(relay_y, 1)
    run(relay_far, 1)
    run(relay_y, 2)
    run(relay_far, 2)
    run(relay_opp, 0)
    scattered(0)
    attend_group(0, 0)
    run(relay_opp, 3)
    scatter_q(1)
    attend_group(0, 1)
    run(relay_opp, 1)
    attend_group(0, 2)
    run(relay_opp, 2)
    attend_group(0, 3)
    scattered(1)
    attend_group(1, 0)
    run(finish, 0)
    attend_group(1, 1)
    run(finish, 3)
    attend_group(1, 2)
    run(finish, 1)
    attend_group(1, 3)
    run(finish, 2)
    run(from_sibling)
    returned(0, 0, 1, 2, 3)
    project(0, True, False)
    returned(1, 0, 1, 2, 3)
    project(1, False, True)
    if PARTS["gather"]:
        for copy in pending:
            copy.wait_send()
    if PARTS["a2a"]:
        for h in range(heads):
            arrived(sent.at[h, pl.ds(0, 15)], back_send.at[h])
            for t in range(3):
                arrived(qb[h].at[pl.ds(0, 15 * per)], out_sems.at[t, h])
    if PARTS["project"]:
        arrived(outv, own_sem.at[1])


def shards(queries, keys, values, out_weight, block_lists, block_counts):
    groups = lax.axis_size("seq")
    others = lax.axis_size("fsdp")
    head_count = block_counts.shape[1]
    blocks = block_counts.shape[2]
    heads = head_count // groups
    span = queries.shape[1]
    dim = queries.shape[2] // head_count
    depth, width = out_weight.shape
    block = span * groups // blocks
    bf16 = jnp.bfloat16
    dma = pltpu.SemaphoreType.DMA
    hbm = pl.BlockSpec(memory_space=pl.ANY)
    head_buf = pltpu.VMEM((blocks, block, dim), bf16)
    return pl.pallas_call(
        kernel,
        out_shape=jax.ShapeDtypeStruct((1, span, width), bf16),
        in_specs=[hbm] * 6,
        out_specs=hbm,
        scratch_shapes=[
            pltpu.SMEM((heads, blocks, block_lists.shape[3]), jnp.int32),
            pltpu.SMEM((head_count, blocks), jnp.int32),
            *[head_buf] * (2 * heads),
            *[pltpu.VMEM((blocks + 1, block, 2 * dim), bf16)] * heads,
            pltpu.VMEM((heads, groups, span, dim), bf16),
            pltpu.VMEM((span, head_count * dim), bf16),
            pltpu.VMEM((2, 4, 2, others, depth, width), bf16),
            pltpu.VMEM((span, width), jnp.float32),
            pltpu.VMEM((span, width), bf16),
            dma((2, heads)), dma((heads, groups // GROUP)), dma((3, heads)), dma((4,)),
            dma((48,)), dma((48,)), dma((32,)), dma((32,)),
            dma((heads, groups // GROUP)), dma((heads,)),
        ],
        compiler_params=pltpu.CompilerParams(
            collective_id=0, has_side_effects=True, vmem_limit_bytes=60 << 20,
        ),
    )(block_lists, block_counts, *(a.reshape(-1, block, a.shape[2]) for a in (queries, keys, values)), out_weight)


def solution(mesh):
    return jax.shard_map(
        shards,
        mesh=mesh,
        in_specs=(
            P("fsdp", "seq", None),
            P("fsdp", "seq", None),
            P("fsdp", "seq", None),
            P(("seq", "fsdp"), None),
            P("fsdp", None, None, None),
            P("fsdp", None, None),
        ),
        out_specs=P("fsdp", "seq", None),
        check_vma=False,
    )
```

```python
import functools
import math

import jax
import jax.numpy as jnp
from jax import lax
from jax.experimental import pallas as pl
from jax.experimental.pallas import tpu as pltpu
from jax.sharding import PartitionSpec as P

MESH = pl.DeviceIdType.MESH
GROUP = 4
BOTH = (3,)
PARTS = dict(a2a=True, gather=True, attend=True, project=True)


def kernel(
    lists_hbm, counts_hbm, q_hbm, k_hbm, v_hbm, w_hbm, out_hbm,
    lists, counts, q0, q1, k0, k1, v0, v1, sent, rows, wb, acc, outv,
    in_sems, q_sems, out_sems, own_sem, w_recv, w_send, sib_recv, sib_send,
    back_recv, back_send,
):
    seq = lax.axis_index("seq")
    fs = lax.axis_index("fsdp")
    xl, z, c = seq // 8, (seq // 2) % 4, seq % 2
    xh, y = fs // 4, fs % 4
    qb, kb, vb = (q0, q1), (k0, k1), (v0, v1)
    heads, blocks, dim = len(qb), q0.shape[0], q0.shape[2]
    per = q_hbm.shape[0]
    span = per * dim

    def seq_of(a, b, d):
        return (a * 4 + b) * 2 + d

    up, down = xh * 4 + (y + 1) % 4, xh * 4 + (y + 3) % 4
    opp = xh * 4 + (y + 2) % 4
    far = (1 - xh) * 4
    x_peer = (seq_of(1 - xl, z, c), fs)
    far_peer = (seq_of(1 - xl, z, c), far + y)
    sibling = (seq_of(xl, z, 1 - c), fs)
    z_up, z_down = (z + 1) % 4, (z + 3) % 4
    z_opp = (z + 2) % 4
    up_peer, down_peer = (seq, up), (seq, down)

    barrier = pltpu.get_barrier_semaphore()
    for d in range(1, 16):
        pl.semaphore_signal(barrier, inc=1, device_id=((seq + d) % 16, fs), device_id_type=MESH)
    for peer in (far_peer, up_peer, down_peer):
        pl.semaphore_signal(barrier, inc=1, device_id=peer, device_id_type=MESH)
    fetched = [
        pltpu.make_async_copy(lists_hbm.at[0, pl.ds(seq * heads, heads)], lists, own_sem.at[2]),
        pltpu.make_async_copy(counts_hbm.at[0], counts, own_sem.at[3]),
    ]
    own = wb.at[xl, z, c, fs]
    if PARTS["gather"]:
        fetched.append(pltpu.make_async_copy(w_hbm, own, own_sem.at[0]))
    for copy in fetched:
        copy.start()
    for h in range(heads):
        vb[h][:blocks, :, dim:] = jnp.ones((blocks, dim, dim), jnp.bfloat16)
        vb[h][blocks] = jnp.zeros((dim, 2 * dim), jnp.bfloat16)
    for copy in fetched:
        copy.wait()
    pl.semaphore_wait(barrier, 18)

    pending = []

    def send(src, dst, ssem, rsem, peer):
        copy = pltpu.make_async_remote_copy(
            src_ref=src, dst_ref=dst, send_sem=ssem, recv_sem=rsem,
            device_id=peer, device_id_type=MESH,
        )
        copy.start()
        return copy

    def share(view, n, peer):
        pending.append(send(view, view, w_send.at[n], w_recv.at[n], peer))

    def arrived(ref, sem):
        pltpu.make_async_copy(ref, ref, sem).wait()

    def landing(buf, first, count):
        view = buf.at[pl.ds(first, count)]
        return view if buf.shape[2] == dim else view.at[:, :, pl.ds(0, dim)]

    order = [(dx, dz, dc) for dc in (1, 0) for dx in (1, 0) for dz in (2, 1, 3, 0)]

    def peer_at(n, way):
        dx, dz, dc = order[n]
        return seq_of((xl + dx) % 2, (z + 4 + way * dz) % 4, (c + dc) % 2)

    def scatter(hbm, buf, h, out_sem, in_sem, lo, hi):
        if not PARTS["a2a"]:
            return
        mine = landing(buf[h], seq * per, per)
        for n in range(lo, hi):
            p = peer_at(n, 1)
            block = hbm.at[:, :, pl.ds(pl.multiple_of((p * heads + h) * dim, dim), dim)]
            if n < 15:
                send(block, mine, out_sem, in_sem(n), (p, fs))
            else:
                pltpu.make_async_copy(block, mine, in_sem(n)).start()

    def scatter_k(h, lo=0, hi=16):
        scatter(k_hbm, kb, h, out_sems.at[0, h], lambda n: in_sems.at[0, h], lo, hi)

    def scatter_v(h, lo=0, hi=16):
        scatter(v_hbm, vb, h, out_sems.at[1, h], lambda n: in_sems.at[1, h], lo, hi)

    def scatter_q(h, lo=0, hi=16):
        scatter(q_hbm, qb, h, out_sems.at[2, h], lambda n: q_sems.at[h, n // GROUP], lo, hi)

    def scattered(h):
        if PARTS["a2a"]:
            arrived(landing(kb[h], 0, blocks), in_sems.at[0, h])
            arrived(landing(vb[h], 0, blocks), in_sems.at[1, h])

    def queries_in(h, g):
        if PARTS["a2a"]:
            arrived(qb[h].at[pl.ds(0, GROUP * per)], q_sems.at[h, g])

    def pair(d, j):
        return wb.at[:, (z + d) % 4, c, j]

    def to_sibling(d, kind, view):
        n = d * 8 + kind
        pending.append(send(view, view, sib_send.at[n], sib_recv.at[n], sibling))

    def slot(d, kind):
        return 8 + d * 10 + kind

    def blocks_out(d):
        view = pair(d, fs)
        if d > 0:
            for kind, peer in ((0, up_peer), (1, down_peer), (2, far_peer)):
                share(view, slot(d, kind), peer)
        to_sibling(d, 0, view)

    def arrived_pair(d, j, kind, flip):
        if d > 0:
            arrived(pair(d, j), w_recv.at[slot(d, kind)])
        else:
            first = 1 - xl if flip else xl
            arrived(wb.at[first, z, c, j], w_recv.at[5 + kind])
            arrived(wb.at[1 - first, z, c, j], w_recv.at[slot(0, kind)])

    def relay_y(d):
        below, above = pair(d, down), pair(d, up)
        arrived_pair(d, down, 0, False)
        share(below.at[0], slot(d, 3), up_peer)
        if d in BOTH:
            share(below.at[1], slot(d, 8), far_peer)
        to_sibling(d, 1, below)
        arrived_pair(d, up, 1, False)
        share(above.at[1], slot(d, 4), down_peer)
        if d in BOTH:
            share(above.at[0], slot(d, 9), far_peer)
        to_sibling(d, 2, above)

    def relay_far(d):
        across = pair(d, far + y)
        arrived_pair(d, far + y, 2, True)
        share(across.at[0] if d in BOTH else across, slot(d, 5), up_peer)
        share(across.at[1] if d in BOTH else across, slot(d, 6), down_peer)
        to_sibling(d, 3, across)

    def relay_opp(d):
        facing = pair(d, opp)
        arrived(facing.at[0], w_recv.at[slot(d, 3)])
        arrived(facing.at[1], w_recv.at[slot(d, 4)])
        share(facing, slot(d, 7), far_peer)
        to_sibling(d, 4, facing)

    def finish(d):
        low, high, last = (pair(d, far + (y + n) % 4) for n in (3, 1, 2))
        if d in BOTH:
            arrived(low.at[0], w_recv.at[slot(d, 5)])
            arrived(low.at[1], w_recv.at[slot(d, 8)])
            arrived(high.at[1], w_recv.at[slot(d, 6)])
            arrived(high.at[0], w_recv.at[slot(d, 9)])
        else:
            arrived(low, w_recv.at[slot(d, 5)])
            arrived(high, w_recv.at[slot(d, 6)])
        to_sibling(d, 5, low)
        to_sibling(d, 6, high)
        arrived(last, w_recv.at[slot(d, 7)])
        to_sibling(d, 7, last)

    def z_peer(zz):
        return (seq_of(xl, zz, c), fs)

    def gather_own():
        share(own, 0, x_peer)
        for kind, peer in ((0, up_peer), (1, down_peer), (2, far_peer)):
            share(own, 5 + kind, peer)

    def gather_x():
        other = wb.at[1 - xl, z, c, fs]
        arrived(other, w_recv.at[0])
        share(pair(0, fs), 1, z_peer(z_up))
        share(pair(0, fs), 2, z_peer(z_down))
        for kind, peer in ((0, up_peer), (1, down_peer), (2, far_peer)):
            share(other, slot(0, kind), peer)
        blocks_out(0)

    def gather_z():
        arrived(pair(3, fs), w_recv.at[1])
        share(wb.at[0, z_down, c, fs], 3, z_peer(z_up))
        arrived(pair(1, fs), w_recv.at[2])
        share(wb.at[1, z_up, c, fs], 4, z_peer(z_down))
        blocks_out(3)
        blocks_out(1)

    def gather_opp():
        arrived(wb.at[0, z_opp, c, fs], w_recv.at[3])
        arrived(wb.at[1, z_opp, c, fs], w_recv.at[4])
        blocks_out(2)

    def run(step, *args):
        if PARTS["gather"]:
            step(*args)

    scale = dim ** -0.5 * math.log2(math.e)

    def attend(h, i):
        live = counts[seq * heads + h, i]
        first = lists[h, i, 0]
        ids = [lists[h, i, j] for j in range(8)]
        key_ids = [jnp.where(j < live, ids[j], first) for j in range(8)]
        value_ids = [jnp.where(j < live, ids[j], blocks) for j in range(8)]
        q = qb[h][i]
        scores = []
        for j in range(0, 8, 2):
            keys = jnp.concatenate([kb[h][key_ids[j]], kb[h][key_ids[j + 1]]], axis=0)
            scores.append(lax.dot_general(q, keys, (((1,), (1,)), ((), ())), preferred_element_type=jnp.float32))
        top = jnp.maximum(jnp.maximum(scores[0], scores[1]), jnp.maximum(scores[2], scores[3]))
        top = jnp.max(jnp.maximum(top[:, :dim], top[:, dim:]), axis=1, keepdims=True)
        mixed = None
        for j in range(0, 8, 2):
            weights = jnp.exp2((scores[j // 2] - top) * scale).astype(jnp.bfloat16)
            values = jnp.concatenate([vb[h][value_ids[j]], vb[h][value_ids[j + 1]]], axis=0)
            part = jnp.dot(weights, values, preferred_element_type=jnp.float32)
            mixed = part if mixed is None else mixed + part
        return (mixed[:, :dim] / mixed[:, dim:]).astype(jnp.bfloat16)

    def attend_group(h, g):
        if not PARTS["a2a"]:
            return
        queries_in(h, g)
        peers = [peer_at(g * GROUP + n, -1) for n in range(GROUP)]
        if PARTS["attend"]:
            done = [[attend(h, p * per + part) for part in range(per)] for p in peers]
            for p, blocks_of in zip(peers, done):
                for part in range(per):
                    sent[h, p, pl.ds(part * dim, dim), :] = blocks_of[part]
        columns = pl.ds(pl.multiple_of((h * 16 + seq) * dim, dim), dim)
        for n, p in enumerate(peers):
            if g * GROUP + n < 15:
                send(sent.at[h, p], rows.at[:, columns], back_send.at[h], back_recv.at[h, g], (p, fs))
            else:
                pltpu.make_async_copy(sent.at[h, p], rows.at[:, columns], back_recv.at[h, g]).start()

    def returned(h, *groups):
        if PARTS["a2a"]:
            for g in groups:
                arrived(rows.at[:, pl.ds(0, GROUP * dim)], back_recv.at[h, g])

    def from_sibling():
        for d in range(4):
            for kind, j in enumerate((
                fs, down, up, far + y, opp, far + (y + 3) % 4, far + (y + 1) % 4, far + (y + 2) % 4,
            )):
                arrived(wb.at[:, (z + d) % 4, 1 - c, j], sib_recv.at[d * 8 + kind])

    chunk = 1024
    others, depth = wb.shape[3], wb.shape[4]

    def project(h, first, last):
        if not PARTS["project"]:
            return
        near = pl.ds(h * dim // depth, dim // depth)

        def body(n, carry):
            cols = pl.ds(pl.multiple_of(n * chunk, chunk), chunk)
            part = jnp.dot(
                rows[:, h * 16 * dim:(h + 1) * 16 * dim],
                wb[:, :, :, near, :, cols].reshape(16 * dim, chunk), preferred_element_type=jnp.float32,
            )
            if not first:
                part = acc[:, cols] + part
            if last:
                outv[:, cols] = part.astype(jnp.bfloat16)
                pltpu.make_async_copy(outv.at[:, cols], out_hbm.at[0, :, cols], own_sem.at[1]).start()
            else:
                acc[:, cols] = part
            return carry

        lax.fori_loop(0, outv.shape[1] // chunk, body, 0)

    run(gather_own)
    scatter_k(0)
    run(gather_x)
    scatter_v(0, 0, 8)
    run(gather_z)
    scatter_v(0, 8, 16)
    run(gather_opp)
    scatter_q(0)
    run(relay_y, 0)
    run(relay_far, 0)
    scatter_k(1)
    scatter_v(1)
    run(relay_y, 3)
    run(relay_far, 3)
    run(relay_y, 1)
    run(relay_far, 1)
    run(relay_y, 2)
    run(relay_far, 2)
    run(relay_opp, 0)
    scattered(0)
    attend_group(0, 0)
    run(relay_opp, 3)
    scatter_q(1)
    attend_group(0, 1)
    run(relay_opp, 1)
    attend_group(0, 2)
    run(relay_opp, 2)
    attend_group(0, 3)
    scattered(1)
    attend_group(1, 0)
    run(finish, 0)
    attend_group(1, 1)
    run(finish, 3)
    attend_group(1, 2)
    run(finish, 1)
    attend_group(1, 3)
    run(finish, 2)
    run(from_sibling)
    returned(0, 0, 1, 2, 3)
    project(0, True, False)
    returned(1, 0, 1, 2, 3)
    project(1, False, True)
    if PARTS["gather"]:
        for copy in pending:
            copy.wait_send()
    if PARTS["a2a"]:
        for h in range(heads):
            arrived(sent.at[h, pl.ds(0, 15)], back_send.at[h])
            for t in range(3):
                arrived(qb[h].at[pl.ds(0, 15 * per)], out_sems.at[t, h])
    if PARTS["project"]:
        arrived(outv, own_sem.at[1])


def shards(queries, keys, values, out_weight, block_lists, block_counts):
    groups = lax.axis_size("seq")
    others = lax.axis_size("fsdp")
    head_count = block_counts.shape[1]
    blocks = block_counts.shape[2]
    heads = head_count // groups
    span = queries.shape[1]
    dim = queries.shape[2] // head_count
    depth, width = out_weight.shape
    block = span * groups // blocks
    bf16 = jnp.bfloat16
    dma = pltpu.SemaphoreType.DMA
    hbm = pl.BlockSpec(memory_space=pl.ANY)
    head_buf = pltpu.VMEM((blocks, block, dim), bf16)
    return pl.pallas_call(
        kernel,
        out_shape=jax.ShapeDtypeStruct((1, span, width), bf16),
        in_specs=[hbm] * 6,
        out_specs=hbm,
        scratch_shapes=[
            pltpu.SMEM((heads, blocks, block_lists.shape[3]), jnp.int32),
            pltpu.SMEM((head_count, blocks), jnp.int32),
            *[head_buf] * (2 * heads),
            *[pltpu.VMEM((blocks + 1, block, 2 * dim), bf16)] * heads,
            pltpu.VMEM((heads, groups, span, dim), bf16),
            pltpu.VMEM((span, head_count * dim), bf16),
            pltpu.VMEM((2, 4, 2, others, depth, width), bf16),
            pltpu.VMEM((span, width), jnp.float32),
            pltpu.VMEM((span, width), bf16),
            dma((2, heads)), dma((heads, groups // GROUP)), dma((3, heads)), dma((4,)),
            dma((48,)), dma((48,)), dma((32,)), dma((32,)),
            dma((heads, groups // GROUP)), dma((heads,)),
        ],
        compiler_params=pltpu.CompilerParams(
            collective_id=0, has_side_effects=True, vmem_limit_bytes=60 << 20,
        ),
    )(block_lists, block_counts, *(a.reshape(-1, block, a.shape[2]) for a in (queries, keys, values)), out_weight)


def solution(mesh):
    return jax.shard_map(
        shards,
        mesh=mesh,
        in_specs=(
            P("fsdp", "seq", None),
            P("fsdp", "seq", None),
            P("fsdp", "seq", None),
            P(("seq", "fsdp"), None),
            P("fsdp", None, None, None),
            P("fsdp", None, None),
        ),
        out_specs=P("fsdp", "seq", None),
        check_vma=False,
    )
```
